32 devices in a mesh: seq: 4 (over x, core), shard: 8 (over z, y).
Axes of the slice: x: 2, y: 2, z: 4, core: 2. Of those that a mesh axis runs over, the one named last changes fastest.
Arguments:
- hidden_in: float32 [16, 1024, 768], P('shard', 'seq'), may hold values from -6 to 6
- doc_starts: int32 [16, 8], P('shard'), may hold values from 0 to 1023, as said below
- query_weight: float32 [768, 768], P('shard'), may hold values from -0.21875 to 0.21875
- query_bias: float32 [768], P('shard'), may hold values from -3 to 3
- key_weight: float32 [768, 768], P('shard'), may hold values from -0.21875 to 0.21875
- value_weight: float32 [768, 768], P('shard'), may hold values from -0.21875 to 0.21875
- value_bias: float32 [768], P('shard'), may hold values from -1 to 1
- out_weight: float32 [768, 768], P('shard'), may hold values from -0.875 to 0.875
- out_bias: float32 [768], P('shard'), may hold values from -2 to 2
- first_gain: float32 [768], P('shard'), may hold values from 0.25 to 1.75
- first_shift: float32 [768], P('shard'), may hold values from -2 to 2
- up_weight: float32 [768, 3072], P('shard'), may hold values from -0.21875 to 0.21875
- up_bias: float32 [3072], P('shard'), may hold values from -3 to 3
- down_weight: float32 [3072, 768], P('shard'), may hold values from -0.109375 to 0.109375
- down_bias: float32 [768], P('shard'), may hold values from -2 to 2
- second_gain: float32 [768], P('shard'), may hold values from 0.25 to 1.75
- second_shift: float32 [768], P('shard'), may hold values from -2 to 2
- grad_out: float32 [16, 1024, 768], P('shard', 'seq'), may hold values from -6 to 6
Outputs:
- hidden_out: float32 [16, 1024, 768], P('shard', 'seq')
- grad_in: float32 [16, 1024, 768], P('shard', 'seq')
- grad_query_weight: float32 [768, 768], P('shard')
- grad_query_bias: float32 [768], P('shard')
- grad_key_weight: float32 [768, 768], P('shard')
- grad_value_weight: float32 [768, 768], P('shard')
- grad_value_bias: float32 [768], P('shard')
- grad_out_weight: float32 [768, 768], P('shard')
- grad_out_bias: float32 [768], P('shard')
- grad_first_gain: float32 [768], P('shard')
- grad_first_shift: float32 [768], P('shard')
- grad_up_weight: float32 [768, 3072], P('shard')
- grad_up_bias: float32 [3072], P('shard')
- grad_down_weight: float32 [3072, 768], P('shard')
- grad_down_bias: float32 [768], P('shard')
- grad_second_gain: float32 [768], P('shard')
- grad_second_shift: float32 [768], P('shard')
The draws below stay inside these ranges and needn't reach their ends.
Inputs may be any that keep to these rules, and one draw needn't show every extreme that they name: doc_starts[s, 0] is 0 and each row rises strictly; document j of sequence s holds the positions from doc_starts[s, j] up to the next start (or 1024) less one.
All inputs are finite; a program needn't handle non-finite values.
Results may differ from the reference program's by a relative error of at most 0.014.
The reference program's roundings to bfloat16 on the way count: a program that leaves them out, or rounds other values in their place, can miss the bound.
Values may be sent and summed in bfloat16 or wider, within the bound.
No kernel may reach another device: no remote copies, remote signals or barrier semaphores. Data moves between devices by JAX's collectives and lax.ppermute only.
A program may use at most 192 MiB of HBM per device.

```python
import math
import jax
import jax.numpy as jnp
from jax import lax

D = 768
H = 12
HD = 64
FF = 3072
LEN = 1024
NDOC = 8
SEQS = 16


def draw_doc_starts(key, part):

    def one_row(row_key):
        order = jax.random.permutation(row_key, LEN - 1) + 1
        chosen = jnp.sort(order[:NDOC - 1]).astype(jnp.int32)
        return jnp.concatenate([jnp.zeros((1,), jnp.int32), chosen])
    row_keys = jax.random.split(jax.random.fold_in(key, 11), SEQS)
    table = jax.vmap(one_row)(row_keys)
    return table.at[0, NDOC - 1].set(LEN - 1)


def raised(values, key, source, target, blocks, factor):
    def block_of(axis_at):
        return (jnp.arange(values.shape[axis_at]) // (values.shape[axis_at] // blocks)).reshape((-1,) + (1,) * (values.ndim - 1 - axis_at))

    one_side = jax.random.permutation(key, blocks)[block_of(target)]
    far = (block_of(target) + blocks // 2) % blocks
    return jnp.where((block_of(source) == one_side) | (block_of(source) == far), factor * values, values)


def level_of(rng, extent, cuts, least, high):
    level, own = 1.0, jax.random.fold_in(rng, 6)
    for dim, parts in cuts:
        steps = jnp.exp(jax.random.uniform(jax.random.fold_in(own, dim), (parts,), jnp.float32, least / len(cuts), high / len(cuts)))
        level = level * jnp.repeat(steps, extent[dim] // parts).reshape([-1 if axis == dim else 1 for axis in range(len(extent))])
    return level


def gaussian(key, shape, scale, reach, cuts=(), kind=jnp.bfloat16):
    entries = jax.random.normal(key, shape, jnp.float32) * scale
    if len(cuts) > 0:
        entries = level_of(key, shape, cuts, -0.22, 0.18) * entries
    return jnp.clip(entries, min=-reach, max=reach).astype(kind)


def gaussian_with(key, extent, width, bound, cuts, heavy, kind=jnp.bfloat16):
    values = width * jax.random.normal(key, extent, jnp.float32)
    if cuts:
        values = values * level_of(key, extent, cuts, -0.22, 0.18)
    return jnp.clip(raised(values, jax.random.fold_in(key, 3), *heavy), -bound, bound).astype(kind)


def setup_inputs(seed: int = 0) -> dict:
    key_of = jax.random.split(jax.random.key(seed), 19)
    hidden_in = gaussian(key_of[0], (SEQS, LEN, D), 1.0, 6.0, ((0, 8), (1, 4)), jnp.float32)
    doc_starts = draw_doc_starts(jax.random.fold_in(key_of[18], 71), 0)
    query_weight = gaussian(key_of[2], (D, D), D ** -0.5, 0.21875, ((0, 8),), jnp.float32)
    query_bias = gaussian(key_of[3], (D,), 0.5, 3.0, ((0, 8),), jnp.float32)
    key_weight = gaussian(key_of[4], (D, D), D ** -0.5, 0.21875, ((0, 8),), jnp.float32)
    value_weight = gaussian(key_of[5], (D, D), D ** -0.5, 0.21875, ((0, 8),), jnp.float32)
    value_bias = gaussian(key_of[6], (D,), 0.15, 1.0, ((0, 8),), jnp.float32)
    out_weight = gaussian(key_of[7], (D, D), (D // 16) ** -0.5, 0.875, ((0, 8),), jnp.float32)
    out_bias = gaussian(key_of[8], (D,), 0.3, 2.0, ((0, 8),), jnp.float32)
    first_gain = jnp.clip(1.0 + 0.15 * jax.random.normal(key_of[9], (D,), jnp.float32), 0.25, 1.75)
    first_shift = gaussian(key_of[10], (D,), 0.3, 2.0, ((0, 8),), jnp.float32)
    up_weight = gaussian(key_of[11], (D, FF), D ** -0.5, 0.21875, ((0, 8),), jnp.float32)
    up_bias = gaussian(key_of[12], (FF,), 0.5, 3.0, ((0, 8),), jnp.float32)
    down_weight = gaussian(key_of[13], (FF, D), FF ** -0.5, 0.109375, ((0, 8),), jnp.float32)
    down_bias = gaussian(key_of[14], (D,), 0.3, 2.0, ((0, 8),), jnp.float32)
    second_gain = jnp.clip(1.0 + 0.15 * jax.random.normal(key_of[15], (D,), jnp.float32), 0.25, 1.75)
    second_shift = gaussian(key_of[16], (D,), 0.3, 2.0, ((0, 8),), jnp.float32)
    grad_out = gaussian_with(key_of[17], (SEQS, LEN, D), 1.0, 6.0, ((0, 8), (1, 4)), (0, 2, 8, 2.0), jnp.float32)
    return {"hidden_in": hidden_in, "doc_starts": doc_starts, "query_weight": query_weight, "query_bias": query_bias, "key_weight": key_weight, "value_weight": value_weight, "value_bias": value_bias, "out_weight": out_weight, "out_bias": out_bias, "first_gain": first_gain, "first_shift": first_shift, "up_weight": up_weight, "up_bias": up_bias, "down_weight": down_weight, "down_bias": down_bias, "second_gain": second_gain, "second_shift": second_shift, "grad_out": grad_out}


@jax.custom_vjp
def low(v):
    return lax.optimization_barrier(v.astype(jnp.bfloat16)).astype(jnp.float32)

@jax.custom_vjp
def low_back(v):
    return v

def low_keep(v):
    return (low(v), None)

def low_pass(kept, grad):
    return (grad,)

def back_keep(v):
    return (v, None)

def back_low(kept, grad):
    return (low(grad),)
low.defvjp(low_keep, low_pass)
low_back.defvjp(back_keep, back_low)
NORM_EPS = 1e-12
NEG_FILL = -1e+30
ROOT_HALF = 0.7071067811865476

def matmul_high(left_side, right_side):
    return jnp.matmul(left_side, right_side, precision=lax.Precision.HIGHEST)

def layer_norm(inputs, norm_gain, norm_shift):
    average = lax.optimization_barrier(jnp.mean(inputs, axis=-1, keepdims=True))
    centered = inputs - average
    variance = lax.optimization_barrier(jnp.mean(centered * centered, axis=-1, keepdims=True))
    return centered * lax.rsqrt(variance + NORM_EPS) * norm_gain + norm_shift

def gelu_value(inputs):
    return 0.5 * inputs * (1.0 + jax.scipy.special.erf(inputs * ROOT_HALF))

def document_ids(starts, length):
    places = jnp.arange(length, dtype=jnp.int32)
    return lax.optimization_barrier(jnp.sum((starts[:, None, :] <= places[None, :, None]).astype(jnp.int32), axis=2))

def attend_sequence(query_heads, key_heads, value_heads, doc_ids):
    block_rows = min(512, LEN)
    block_count = LEN // block_rows
    score_scale = HD ** (-0.5)

    def one_block(pieces):
        query_block, doc_block = pieces
        scores = jnp.einsum('qhd,khd->hqk', query_block, key_heads, precision=lax.Precision.HIGHEST) * score_scale
        scores = low_back(scores)
        allowed = doc_block[:, None] == doc_ids[None, :]
        scores = jnp.where(allowed[None], scores, NEG_FILL)
        highest = lax.optimization_barrier(jnp.max(scores, axis=-1, keepdims=True))
        exponent = jnp.exp(scores - highest)
        attention = exponent / lax.optimization_barrier(jnp.sum(exponent, axis=-1, keepdims=True))
        return jnp.einsum('hqk,khd->qhd', low(attention), value_heads, precision=lax.Precision.HIGHEST)
    context = lax.map(jax.checkpoint(one_block), (query_heads.reshape(block_count, block_rows, H, HD), doc_ids.reshape(block_count, block_rows)))
    return context.reshape(LEN, H, HD)

def layer_forward(block_in, starts, params):
    rounded = [low(weight_item) for weight_item in params]
    query_matrix, query_offset, key_matrix, value_matrix, value_offset, out_matrix, out_offset, first_scale, first_offset, up_matrix, up_offset, down_matrix, down_offset, second_scale, second_offset = rounded
    group_size = block_in.shape[0]
    token_rows = block_in.reshape(group_size * LEN, D)
    rows_low = low(token_rows)
    queries = low_back(low(matmul_high(rows_low, query_matrix) + query_offset))
    keys_all = low_back(low(matmul_high(rows_low, key_matrix)))
    values_all = low_back(low(matmul_high(rows_low, value_matrix) + value_offset))
    doc_ids = document_ids(starts, LEN)
    context = jax.vmap(attend_sequence)(queries.reshape(group_size, LEN, H, HD), keys_all.reshape(group_size, LEN, H, HD), values_all.reshape(group_size, LEN, H, HD), doc_ids)
    context = low_back(low(context.reshape(group_size * LEN, D)))
    attended = low_back(matmul_high(context, out_matrix) + out_offset)
    normed = layer_norm(token_rows + attended, first_scale, first_offset)
    up_values = low_back(matmul_high(low(normed), up_matrix) + up_offset)
    activated = low(gelu_value(up_values))
    down_values = low_back(matmul_high(activated, down_matrix) + down_offset)
    result = layer_norm(normed + down_values, second_scale, second_offset)
    return result.reshape(group_size, LEN, D)

def reference(hidden_in, doc_starts, query_weight, query_bias, key_weight, value_weight, value_bias, out_weight, out_bias, first_gain, first_shift, up_weight, up_bias, down_weight, down_bias, second_gain, second_shift, grad_out):
    weights = (query_weight, query_bias, key_weight, value_weight, value_bias, out_weight, out_bias, first_gain, first_shift, up_weight, up_bias, down_weight, down_bias, second_gain, second_shift)
    group_size = math.gcd(SEQS, max(1, 4096 // LEN))
    steps_count = SEQS // group_size

    def one_group(totals, inputs):
        block_in, starts, block_grad = inputs

        def forward(values_in, params):
            return layer_forward(values_in, starts, params)
        output, pullback = jax.vjp(forward, block_in, weights)
        grad_inputs, grad_params = pullback(block_grad)
        totals = tuple((running + added for running, added in zip(totals, grad_params)))
        return (totals, (output, grad_inputs))
    initial = tuple((jnp.zeros_like(weight_item) for weight_item in weights))
    totals, (outputs, grad_inputs) = lax.scan(one_group, initial, (hidden_in.reshape(steps_count, group_size, LEN, D), doc_starts.reshape(steps_count, group_size, NDOC), grad_out.reshape(steps_count, group_size, LEN, D)))
    return (outputs.reshape(SEQS, LEN, D), grad_inputs.reshape(SEQS, LEN, D), totals[0], totals[1], totals[2], totals[3], totals[4], totals[5], totals[6], totals[7], totals[8], totals[9], totals[10], totals[11], totals[12], totals[13], totals[14])
```

```python
import functools

import jax
import jax.numpy as jnp
from jax import lax
from jax.sharding import PartitionSpec as P

HD = 64


NORM_EPS = 1e-12
NEG_FILL = -1e30
ROOT_HALF = 0.7071067811865476
INV_ROOT_TAU = 0.3989422804014327


def product(left_side, right_side):
    return jnp.dot(left_side, right_side, preferred_element_type=jnp.float32)


def product_back(incoming, matrix):
    return jnp.einsum("tj,ij->ti", incoming, matrix, preferred_element_type=jnp.float32)


def weight_grad(left_side, incoming):
    return jnp.einsum("ti,tj->ij", left_side, incoming, preferred_element_type=jnp.float32)


def column_sum(incoming):
    return jnp.sum(incoming.astype(jnp.float32), axis=0)


def gelu_value(inputs):
    return 0.5 * inputs * (1.0 + jax.scipy.special.erf(inputs * ROOT_HALF))


def gelu_slope(inputs):
    return 0.5 * (
        1.0 + jax.scipy.special.erf(inputs * ROOT_HALF)
    ) + inputs * INV_ROOT_TAU * jnp.exp(-0.5 * inputs * inputs)


def norm_forward(inputs, norm_gain, norm_shift):
    average = jnp.mean(inputs, axis=-1, keepdims=True)
    centered = inputs - average
    variance = jnp.mean(centered * centered, axis=-1, keepdims=True)
    inv_root = lax.rsqrt(variance + NORM_EPS)
    unit_rows = centered * inv_root
    return (unit_rows * norm_gain + norm_shift, unit_rows, inv_root)


def norm_backward(incoming, unit_rows, inv_root, norm_gain):
    scaled = incoming * norm_gain
    grad_input = inv_root * (
        scaled
        - jnp.mean(scaled, axis=-1, keepdims=True)
        - unit_rows * jnp.mean(scaled * unit_rows, axis=-1, keepdims=True)
    )
    return (grad_input, jnp.sum(incoming * unit_rows, axis=0), jnp.sum(incoming, axis=0))


def document_ids(starts, length):
    places = jnp.arange(length, dtype=jnp.int32)
    return jnp.sum((starts[:, None, :] <= places[None, :, None]).astype(jnp.int32), axis=2)


def masked_scores(query_block, key_heads, doc_block, doc_ids, score_scale):
    scores = (
        jnp.einsum("qhd,khd->hqk", query_block, key_heads, preferred_element_type=jnp.float32)
        * score_scale
    )
    allowed = doc_block[:, None] == doc_ids[None, :]
    return jnp.where(allowed[None], scores, NEG_FILL)


def flip_core(value):
    return lax.ppermute(value, "seq", [(s, s ^ 1) for s in range(4)])


def flip_x(value):
    return lax.ppermute(value, "seq", [(s, s ^ 2) for s in range(4)])


def shard_factors(count):
    if count == 8:
        return (4, 2)
    if count == 64:
        return (2, 8, 4)
    return (count,)


def factor_strides(factors):
    strides = []
    step = 1
    for size in reversed(factors):
        strides.insert(0, step)
        step *= size
    return tuple(strides)


def flip_shard(value, count, stride, offset):
    return lax.ppermute(value, "shard", [(h, h ^ (offset * stride)) for h in range(count)])


def place_pair(own, other, high, axis):
    return jnp.where(
        high, jnp.concatenate([other, own], axis), jnp.concatenate([own, other], axis)
    )


def gather_shard(piece, count):
    factors = shard_factors(count)
    strides = factor_strides(factors)
    index = lax.axis_index("shard")
    gathered = piece[None]
    for size, stride in zip(factors, strides):
        place = (index // stride) % size
        block = jnp.zeros((gathered.shape[0], size) + piece.shape, piece.dtype)
        for offset in range(size):
            came = gathered if offset == 0 else flip_shard(gathered, count, stride, offset)
            block = lax.dynamic_update_slice_in_dim(block, came[:, None], place ^ offset, 1)
        gathered = block.reshape((gathered.shape[0] * size,) + piece.shape)
    return gathered


def half_of(value, which, axis):
    size = value.shape[axis] // 2
    return lax.dynamic_slice_in_dim(value, which * size, size, axis)


def gather_weight(shard_rows, count, core, across, share_x):
    piece = half_of(shard_rows, core, 1)
    if share_x:
        piece = half_of(piece, across, 1)
    whole = gather_shard(piece, count)
    whole = whole.reshape((-1, whole.shape[-1]))
    if share_x:
        whole = place_pair(whole, flip_x(whole), across == 1, 1)
    return place_pair(whole, flip_core(whole), core == 1, 1)


def add_low(first, *others):
    total = first.astype(jnp.float32)
    for item in others:
        total = total + item.astype(jnp.float32)
    return total.astype(first.dtype)


def reduce_weight(grad, count, core, across, x_first):
    factors = shard_factors(count)
    strides = factor_strides(factors)
    index = lax.axis_index("shard")
    rows, columns = grad.shape
    low = grad.astype(jnp.bfloat16).reshape(factors + (rows // count, columns))
    axis = len(factors)

    def over_x(value):
        row_axis = value.ndim - 2
        return add_low(
            half_of(value, across, row_axis), flip_x(half_of(value, 1 - across, row_axis))
        )

    low = add_low(
        half_of(low, core, axis + 1), flip_core(half_of(low, 1 - core, axis + 1))
    )
    if x_first:
        low = over_x(low)
    for level in reversed(range(len(factors))):
        size, stride = factors[level], strides[level]
        place = (index // stride) % size
        low = add_low(
            lax.dynamic_index_in_dim(low, place, level, False),
            *[
                flip_shard(
                    lax.dynamic_index_in_dim(low, place ^ offset, level, False),
                    count,
                    stride,
                    offset,
                )
                for offset in range(1, size)
            ],
        )
        if level == len(factors) - 1 and not x_first:
            low = over_x(low)
    low = place_pair(low, flip_x(low), across == 1, 0)
    low = place_pair(low, flip_core(low), core == 1, 1)
    return low.astype(jnp.float32)


def reduce_vector(vector, count):
    vector = vector + flip_core(vector)
    vector = vector + flip_x(vector)
    factors = shard_factors(count)
    for size, stride in zip(factors, factor_strides(factors)):
        pieces = [vector] + [
            flip_shard(vector, count, stride, offset) for offset in range(1, size)
        ]
        while len(pieces) > 1:
            pieces = [pieces[i] + pieces[i + 1] for i in range(0, len(pieces), 2)]
        vector = pieces[0]
    return vector


def attend_forward(query_heads, key_heads, value_heads, query_docs, key_docs):
    score_scale = HD ** (-0.5)
    scores = masked_scores(query_heads, key_heads, query_docs, key_docs, score_scale)
    highest = jnp.max(scores, axis=-1, keepdims=True)
    exponent = jnp.exp(scores - highest)
    denominator = jnp.sum(exponent, axis=-1, keepdims=True)
    probs_low = (exponent / denominator).astype(jnp.bfloat16)
    context = jnp.einsum(
        "hqk,khd->qhd", probs_low, value_heads, preferred_element_type=jnp.float32
    )
    return (context.astype(jnp.bfloat16), highest + jnp.log(denominator))


def attend_backward(
    query_heads, key_heads, value_heads, grad_heads, log_total, query_docs, key_docs
):
    score_scale = HD ** (-0.5)
    scores = masked_scores(query_heads, key_heads, query_docs, key_docs, score_scale)
    attention = jnp.exp(scores - log_total)
    grad_attention = jnp.einsum(
        "qhd,khd->hqk", grad_heads, value_heads, preferred_element_type=jnp.float32
    )
    row_inner = jnp.sum(attention * grad_attention, axis=-1, keepdims=True)
    grad_scores = (attention * (grad_attention - row_inner)).astype(jnp.bfloat16)
    grad_query = (
        jnp.einsum("hqk,khd->qhd", grad_scores, key_heads, preferred_element_type=jnp.float32)
        * score_scale
    )
    grad_keys = (
        jnp.einsum("hqk,qhd->khd", grad_scores, query_heads, preferred_element_type=jnp.float32)
        * score_scale
    )
    grad_values = jnp.einsum(
        "hqk,qhd->khd",
        attention.astype(jnp.bfloat16),
        grad_heads,
        preferred_element_type=jnp.float32,
    )
    return (grad_query.astype(jnp.bfloat16), grad_keys, grad_values)


def body(
    hidden_in,
    doc_starts,
    query_weight,
    query_bias,
    key_weight,
    value_weight,
    value_bias,
    out_weight,
    out_bias,
    first_gain,
    first_shift,
    up_weight,
    up_bias,
    down_weight,
    down_bias,
    second_gain,
    second_shift,
    grad_out,
    *,
    count,
):
    low_type = jnp.bfloat16
    wide_type = jnp.float32
    place = lax.axis_index("seq")
    core = place % 2
    across = place // 2
    shard_index = lax.axis_index("shard")
    sequences, part_len, model_width = hidden_in.shape
    full_len = 4 * part_len

    mine = lax.dynamic_index_in_dim(hidden_in, across, 0, False)
    yours = lax.dynamic_index_in_dim(hidden_in, 1 - across, 0, False)
    came_low = flip_x(yours.astype(low_type))
    rows_low = jnp.concatenate([mine.astype(low_type), came_low], 0)
    all_low = jnp.concatenate([rows_low, flip_core(rows_low)], 0)
    rest = flip_x((yours - yours.astype(low_type).astype(wide_type)).astype(low_type))
    token_rows = jnp.concatenate(
        [mine, came_low.astype(wide_type) + rest.astype(wide_type)], 0
    )

    shards = jnp.concatenate([query_weight, key_weight, value_weight], 1).astype(low_type)
    joined = gather_weight(shards, count, core, across, False)
    vectors = (
        query_bias, value_bias, out_bias, first_gain, first_shift,
        down_bias, second_gain, second_shift,
    )
    packed = jnp.stack([item.astype(low_type) for item in vectors])
    packed = jnp.concatenate([packed, up_bias.astype(low_type).reshape(4, -1)], 0)
    packed = gather_shard(packed, count)
    vector_rows = [
        packed[:, i].reshape(-1).astype(wide_type) for i in range(len(vectors))
    ]
    (
        query_offset, value_offset, out_offset, first_scale, first_offset,
        down_offset, second_scale, second_offset,
    ) = vector_rows
    up_offset = packed[:, len(vectors):].reshape(-1).astype(wide_type)
    out_matrix = gather_weight(out_weight.astype(low_type), count, core, across, False)
    up_matrix = gather_weight(up_weight.astype(low_type), count, core, across, True)
    down_matrix = gather_weight(down_weight.astype(low_type), count, core, across, False)

    grad_mine = lax.dynamic_index_in_dim(grad_out, across, 0, False)
    grad_yours = lax.dynamic_index_in_dim(grad_out, 1 - across, 0, False)
    incoming = jnp.concatenate([grad_mine, flip_x(grad_yours)], 0)

    query_matrix = joined[:, :model_width]
    key_matrix = joined[:, model_width : 2 * model_width]
    value_matrix = joined[:, 2 * model_width :]
    query_rows = (product(rows_low, query_matrix) + query_offset).astype(low_type)
    key_rows = product(all_low, key_matrix).astype(low_type)
    value_rows = (product(all_low, value_matrix) + value_offset).astype(low_type)

    heads = model_width // HD
    starts = lax.dynamic_index_in_dim(doc_starts, across, 0, True)
    doc_ids = document_ids(starts, full_len)[0]

    def docs_at(which_core):
        first = lax.dynamic_slice_in_dim(
            doc_ids, (2 * across + which_core) * part_len, part_len
        )
        second = lax.dynamic_slice_in_dim(
            doc_ids, (2 * (1 - across) + which_core) * part_len, part_len
        )
        return jnp.concatenate([first, second])

    query_docs = docs_at(core)
    key_docs = jnp.concatenate([query_docs, docs_at(1 - core)])
    query_heads = query_rows.reshape(-1, heads, HD)
    key_heads = key_rows.reshape(-1, heads, HD)
    value_heads = value_rows.reshape(-1, heads, HD)
    context_heads, log_total = attend_forward(
        query_heads, key_heads, value_heads, query_docs, key_docs
    )
    context_rows = context_heads.reshape(-1, model_width)
    attended = product(context_rows, out_matrix) + out_offset
    normed, unit_one, inv_one = norm_forward(token_rows + attended, first_scale, first_offset)
    normed_low = normed.astype(low_type)
    up_values = product(normed_low, up_matrix) + up_offset
    activated = gelu_value(up_values).astype(low_type)
    down_values = product(activated, down_matrix) + down_offset
    result_rows, unit_two, inv_two = norm_forward(
        normed + down_values, second_scale, second_offset
    )

    def give_back(rows):
        own, other = rows[:part_len], flip_x(rows[part_len:])
        return place_pair(own[None], other[None], across == 1, 0)

    hidden_out = give_back(result_rows)

    grad_sum, grad_second_gain, grad_second_shift = norm_backward(
        incoming, unit_two, inv_two, second_scale
    )
    grad_down = grad_sum.astype(low_type)
    owned_down = reduce_weight(weight_grad(activated, grad_down), count, core, across, True)
    grad_down_bias = column_sum(grad_down)
    grad_up = (product_back(grad_down, down_matrix) * gelu_slope(up_values)).astype(low_type)
    owned_up = reduce_weight(weight_grad(normed_low, grad_up), count, core, across, False)
    grad_up_bias = column_sum(grad_up)
    grad_normed = grad_sum + product_back(grad_up, up_matrix)
    grad_mixed, grad_first_gain, grad_first_shift = norm_backward(
        grad_normed, unit_one, inv_one, first_scale
    )
    grad_attended = grad_mixed.astype(low_type)
    owned_out = reduce_weight(
        weight_grad(context_rows, grad_attended), count, core, across, True
    )
    grad_out_bias = column_sum(grad_attended)
    early = reduce_vector(
        jnp.concatenate(
            [
                grad_second_gain, grad_second_shift, grad_down_bias, grad_first_gain,
                grad_first_shift, grad_out_bias, grad_up_bias,
            ]
        ).reshape(-1, model_width),
        count,
    )
    grad_context = product_back(grad_attended, out_matrix).astype(low_type)
    grad_queries, grad_keys, grad_values = attend_backward(
        query_heads,
        key_heads,
        value_heads,
        grad_context.reshape(-1, heads, HD),
        log_total,
        query_docs,
        key_docs,
    )
    grad_queries = grad_queries.reshape(-1, model_width)
    own_rows = 2 * part_len

    def pair_sum(wide):
        wide = wide.reshape(-1, model_width)
        return (
            wide[:own_rows] + flip_core(wide[own_rows:].astype(low_type)).astype(wide_type)
        ).astype(low_type)

    grad_keys = pair_sum(grad_keys)
    grad_values = pair_sum(grad_values)
    grad_rows = (
        grad_mixed
        + product_back(grad_queries, query_matrix)
        + product_back(grad_keys, key_matrix)
        + product_back(grad_values, value_matrix)
    )
    grad_in = give_back(grad_rows)
    owned_query = reduce_weight(
        weight_grad(rows_low, grad_queries), count, core, across, False
    )
    owned_key = reduce_weight(weight_grad(rows_low, grad_keys), count, core, across, True)
    owned_value = reduce_weight(
        weight_grad(rows_low, grad_values), count, core, across, False
    )
    late = reduce_vector(
        jnp.stack([column_sum(grad_queries), column_sum(grad_values)]), count
    )

    def owned_part(vector):
        size = vector.shape[0] // count
        return lax.dynamic_slice_in_dim(vector, shard_index * size, size)

    return (
        hidden_out,
        grad_in,
        owned_query,
        owned_part(late[0]),
        owned_key,
        owned_value,
        owned_part(late[1]),
        owned_out,
        owned_part(early[5]),
        owned_part(early[3]),
        owned_part(early[4]),
        owned_up,
        owned_part(early[6:].reshape(-1)),
        owned_down,
        owned_part(early[2]),
        owned_part(early[0]),
        owned_part(early[1]),
    )


def solution(mesh):
    placed = (
        P("shard", "seq", None),
        P("shard", None),
        P("shard", None),
        P("shard"),
        P("shard", None),
        P("shard", None),
        P("shard"),
        P("shard", None),
        P("shard"),
        P("shard"),
        P("shard"),
        P("shard", None),
        P("shard"),
        P("shard", None),
        P("shard"),
        P("shard"),
        P("shard"),
        P("shard", "seq", None),
    )
    return jax.shard_map(
        functools.partial(body, count=mesh.shape["shard"]),
        mesh=mesh,
        in_specs=placed,
        out_specs=(
            P("shard", "seq", None),
            P("shard", "seq", None),
            P("shard", None),
            P("shard"),
            P("shard", None),
            P("shard", None),
            P("shard"),
            P("shard", None),
            P("shard"),
            P("shard"),
            P("shard"),
            P("shard", None),
            P("shard"),
            P("shard", None),
            P("shard"),
            P("shard"),
            P("shard"),
        ),
        check_vma=False,
    )
```

```python
import functools

import jax
import jax.numpy as jnp
from jax import lax
from jax.experimental import pallas as pl
from jax.experimental.pallas import tpu as pltpu
from jax.sharding import PartitionSpec as P

HD = 64


NORM_EPS = 1e-12
NEG_FILL = -1e30
ROOT_HALF = 0.7071067811865476
INV_ROOT_TAU = 0.3989422804014327


def product(left_side, right_side):
    return jnp.dot(left_side, right_side, preferred_element_type=jnp.float32)


def product_back(incoming, matrix):
    return jnp.einsum("tj,ij->ti", incoming, matrix, preferred_element_type=jnp.float32)


def weight_grad(left_side, incoming):
    return jnp.einsum("ti,tj->ij", left_side, incoming, preferred_element_type=jnp.float32)


def column_sum(incoming):
    return jnp.sum(incoming.astype(jnp.float32), axis=0)


def gelu_value(inputs):
    return 0.5 * inputs * (1.0 + jax.scipy.special.erf(inputs * ROOT_HALF))


def gelu_slope(inputs):
    return 0.5 * (
        1.0 + jax.scipy.special.erf(inputs * ROOT_HALF)
    ) + inputs * INV_ROOT_TAU * jnp.exp(-0.5 * inputs * inputs)


def norm_forward(inputs, norm_gain, norm_shift):
    average = jnp.mean(inputs, axis=-1, keepdims=True)
    centered = inputs - average
    variance = jnp.mean(centered * centered, axis=-1, keepdims=True)
    inv_root = lax.rsqrt(variance + NORM_EPS)
    unit_rows = centered * inv_root
    return (unit_rows * norm_gain + norm_shift, unit_rows, inv_root)


def norm_backward(incoming, unit_rows, inv_root, norm_gain):
    scaled = incoming * norm_gain
    grad_input = inv_root * (
        scaled
        - jnp.mean(scaled, axis=-1, keepdims=True)
        - unit_rows * jnp.mean(scaled * unit_rows, axis=-1, keepdims=True)
    )
    return (grad_input, jnp.sum(incoming * unit_rows, axis=0), jnp.sum(incoming, axis=0))


def document_ids(starts, length):
    places = jnp.arange(length, dtype=jnp.int32)
    return jnp.sum((starts[:, None, :] <= places[None, :, None]).astype(jnp.int32), axis=2)


def flip_core(value):
    return lax.ppermute(value, "seq", [(s, s ^ 1) for s in range(4)])


def flip_x(value):
    return lax.ppermute(value, "seq", [(s, s ^ 2) for s in range(4)])


def shard_factors(count):
    if count == 8:
        return (4, 2)
    if count == 64:
        return (2, 8, 4)
    return (count,)


def factor_strides(factors):
    strides = []
    step = 1
    for size in reversed(factors):
        strides.insert(0, step)
        step *= size
    return tuple(strides)


def flip_shard(value, count, stride, offset):
    return lax.ppermute(value, "shard", [(h, h ^ (offset * stride)) for h in range(count)])


def place_pair(own, other, high, axis):
    return jnp.where(
        high, jnp.concatenate([other, own], axis), jnp.concatenate([own, other], axis)
    )


def gather_shard(piece, count):
    factors = shard_factors(count)
    strides = factor_strides(factors)
    index = lax.axis_index("shard")
    gathered = piece[None]
    for size, stride in zip(factors, strides):
        place = (index // stride) % size
        block = jnp.zeros((gathered.shape[0], size) + piece.shape, piece.dtype)
        for offset in range(size):
            came = gathered if offset == 0 else flip_shard(gathered, count, stride, offset)
            block = lax.dynamic_update_slice_in_dim(block, came[:, None], place ^ offset, 1)
        gathered = block.reshape((gathered.shape[0] * size,) + piece.shape)
    return gathered


def half_of(value, which, axis):
    size = value.shape[axis] // 2
    return lax.dynamic_slice_in_dim(value, which * size, size, axis)


def gather_weight(shard_rows, count, core, across, share_x):
    piece = half_of(shard_rows, core, 1)
    if share_x:
        piece = half_of(piece, across, 1)
    whole = gather_shard(piece, count)
    whole = whole.reshape((-1, whole.shape[-1]))
    if share_x:
        whole = place_pair(whole, flip_x(whole), across == 1, 1)
    return place_pair(whole, flip_core(whole), core == 1, 1)


def add_low(first, *others):
    total = first.astype(jnp.float32)
    for item in others:
        total = total + item.astype(jnp.float32)
    return total.astype(first.dtype)


def stage_names(count, x_first):
    levels = list(reversed(range(len(shard_factors(count)))))
    if x_first:
        return ["core", "x"] + levels
    return ["core", levels[0], "x"] + levels[1:]


def start_grad(grad, count):
    rows, columns = grad.shape
    return grad.astype(jnp.bfloat16).reshape(shard_factors(count) + (rows // count, columns))


def send_stage(low, stage, count, core, across):
    if stage == "core":
        axis = low.ndim - 1
        return [half_of(low, core, axis), flip_core(half_of(low, 1 - core, axis))]
    if stage == "x":
        axis = low.ndim - 2
        return [half_of(low, across, axis), flip_x(half_of(low, 1 - across, axis))]
    factors = shard_factors(count)
    size, stride = factors[stage], factor_strides(factors)[stage]
    place = (lax.axis_index("shard") // stride) % size
    parts = [lax.dynamic_index_in_dim(low, place, stage, False)]
    for offset in range(1, size):
        part = lax.dynamic_index_in_dim(low, place ^ offset, stage, False)
        parts.append(flip_shard(part, count, stride, offset))
    return parts


def tie(*groups):
    return lax.optimization_barrier(groups)


def spread_owned(owned, core, across):
    flat = []
    for item in owned:
        rows, columns = item.shape
        width = columns // (columns // 384) if columns % 384 == 0 else columns
        for k in range(columns // width):
            flat.append(item[:, k * width : (k + 1) * width])
    packed = jnp.concatenate(flat, 0)
    both = place_pair(packed[None], flip_x(packed)[None], across == 1, 0)
    both = place_pair(both[None], flip_core(both)[None], core == 1, 0)
    results = []
    start = 0
    for item in owned:
        rows, columns = item.shape
        width = columns // (columns // 384) if columns % 384 == 0 else columns
        parts = columns // width
        block = both[:, :, start : start + parts * rows].astype(jnp.float32)
        start += parts * rows
        block = block.reshape(2, 2, parts, rows, width).transpose(1, 3, 0, 2, 4)
        results.append(block.reshape(2 * rows, 2 * columns))
    return results


def reduce_vector(vector, count):
    vector = vector + flip_core(vector)
    vector = vector + flip_x(vector)
    factors = shard_factors(count)
    for size, stride in zip(factors, factor_strides(factors)):
        pieces = [vector] + [
            flip_shard(vector, count, stride, offset) for offset in range(1, size)
        ]
        while len(pieces) > 1:
            pieces = [pieces[i] + pieces[i + 1] for i in range(0, len(pieces), 2)]
        vector = pieces[0]
    return vector


def head_mask(which, width):
    lane = lax.broadcasted_iota(jnp.int32, (1, width), 1)
    return (lane // HD) == which


def transposed_product(left_side, right_side):
    return lax.dot_general(
        left_side, right_side, (((1,), (1,)), ((), ())), preferred_element_type=jnp.float32
    )


def fill_bias(bias_ref, query_docs_ref, key_docs_ref):
    block = pl.program_id(1)

    @pl.when(pl.program_id(0) == 0)
    def _():
        bias_ref[block] = jnp.where(key_docs_ref[...] == query_docs_ref[...], 0.0, NEG_FILL)

    return block


def forward_kernel(
    query_ref, key_ref, value_ref, query_docs_ref, key_docs_ref,
    context_ref, total_ref, bias_ref, flipped_ref,
):
    block = fill_bias(bias_ref, query_docs_ref, key_docs_ref)

    @pl.when(block == 0)
    def _():
        flipped_ref[...] = value_ref[...].T

    query = query_ref[...] * jnp.bfloat16(HD ** (-0.5))
    keys = key_ref[...]
    parts = []
    totals = []
    for which in range(query.shape[1] // HD):
        one = jnp.where(head_mask(which, query.shape[1]), query, jnp.bfloat16(0))
        scores = transposed_product(keys, one) + bias_ref[block]
        highest = jnp.max(scores, axis=0, keepdims=True)
        exponent = jnp.exp(scores - highest)
        denominator = jnp.sum(exponent, axis=0, keepdims=True)
        part = product(
            flipped_ref[which * HD : (which + 1) * HD], exponent.astype(jnp.bfloat16)
        )
        parts.append(part / denominator)
        totals.append(highest + jnp.log(denominator))
    context_ref[...] = jnp.concatenate(parts, 0).T.astype(jnp.bfloat16)
    for which, total in enumerate(totals):
        total_ref[0, which : which + 1] = total


def backward_kernel(
    query_ref, key_ref, value_ref, grad_ref, total_ref, query_docs_ref, key_docs_ref,
    grad_query_ref, own_key_ref, other_key_ref, own_value_ref, other_value_ref,
    bias_ref, flipped_ref, key_sum_ref, value_sum_ref,
):
    block = fill_bias(bias_ref, query_docs_ref, key_docs_ref)

    @pl.when(block == 0)
    def _():
        flipped_ref[...] = key_ref[...].T
        key_sum_ref[...] = jnp.zeros_like(key_sum_ref)
        value_sum_ref[...] = jnp.zeros_like(value_sum_ref)

    query = query_ref[...] * jnp.bfloat16(HD ** (-0.5))
    keys = key_ref[...]
    values = value_ref[...]
    grad = grad_ref[...]
    parts = []
    for which in range(query.shape[1] // HD):
        chosen = head_mask(which, query.shape[1])
        one = jnp.where(chosen, query, jnp.bfloat16(0))
        grad_one = jnp.where(chosen, grad, jnp.bfloat16(0))
        scores = transposed_product(keys, one) + bias_ref[block]
        attention = jnp.exp(scores - total_ref[0, which : which + 1])
        grad_attention = transposed_product(values, grad_one)
        inner = jnp.sum(attention * grad_attention, axis=0, keepdims=True)
        grad_scores = (attention * (grad_attention - inner)).astype(jnp.bfloat16)
        value_sum_ref[...] += product(attention.astype(jnp.bfloat16), grad_one)
        key_sum_ref[...] += product(grad_scores, one)
        parts.append(product(flipped_ref[which * HD : (which + 1) * HD], grad_scores))
    grad_query_ref[...] = (jnp.concatenate(parts, 0).T * HD ** (-0.5)).astype(jnp.bfloat16)

    @pl.when(block == pl.num_programs(1) - 1)
    def _():
        half = own_key_ref.shape[0]
        own_key_ref[...] = key_sum_ref[:half]
        own_value_ref[...] = value_sum_ref[:half]
        other_key_ref[...] = key_sum_ref[half:].astype(jnp.bfloat16)
        other_value_ref[...] = value_sum_ref[half:].astype(jnp.bfloat16)


def attention_specs(rows, keys, block_rows, first):
    query_spec = pl.BlockSpec((block_rows, 2 * HD), lambda p, b: (b, p + first))
    key_spec = pl.BlockSpec((keys, 2 * HD), lambda p, b: (0, p + first))
    total_spec = pl.BlockSpec((1, 8, block_rows), lambda p, b: (p + first, 0, b))
    query_docs_spec = pl.BlockSpec((1, block_rows), lambda p, b: (0, b))
    key_docs_spec = pl.BlockSpec((keys, 1), lambda p, b: (0, 0))
    return query_spec, key_spec, total_spec, query_docs_spec, key_docs_spec


def attend_forward(query_rows, key_rows, value_rows, query_docs, key_docs):
    rows, width = query_rows.shape
    keys = key_rows.shape[0]
    block_rows = min(256, rows)
    blocks = rows // block_rows
    pairs = width // (2 * HD)
    query_spec, key_spec, total_spec, query_docs_spec, key_docs_spec = attention_specs(
        rows, keys, block_rows, 0
    )
    return pl.pallas_call(
        forward_kernel,
        grid=(pairs, blocks),
        in_specs=[query_spec, key_spec, key_spec, query_docs_spec, key_docs_spec],
        out_specs=[query_spec, total_spec],
        out_shape=[
            jax.ShapeDtypeStruct((rows, width), jnp.bfloat16),
            jax.ShapeDtypeStruct((pairs, 8, rows), jnp.float32),
        ],
        scratch_shapes=[
            pltpu.VMEM((blocks, keys, block_rows), jnp.float32),
            pltpu.VMEM((2 * HD, keys), jnp.bfloat16),
        ],
        cost_estimate=pl.CostEstimate(
            flops=16 * rows * keys * width, transcendentals=12 * rows * keys, bytes_accessed=1 << 24
        ),
        name="attend_forward",
    )(query_rows, key_rows, value_rows, query_docs[None], key_docs[:, None])


def attend_backward(
    query_rows, key_rows, value_rows, grad_rows, totals, query_docs, key_docs, first, pairs
):
    rows = query_rows.shape[0]
    keys = key_rows.shape[0]
    block_rows = min(256, rows)
    blocks = rows // block_rows
    width = pairs * 2 * HD
    query_spec, key_spec, total_spec, query_docs_spec, key_docs_spec = attention_specs(
        rows, keys, block_rows, first
    )
    half_spec = pl.BlockSpec((keys // 2, 2 * HD), lambda p, b: (0, p))
    return pl.pallas_call(
        backward_kernel,
        grid=(pairs, blocks),
        in_specs=[
            query_spec, key_spec, key_spec, query_spec, total_spec, query_docs_spec, key_docs_spec,
        ],
        out_specs=[pl.BlockSpec((block_rows, 2 * HD), lambda p, b: (b, p))] + [half_spec] * 4,
        out_shape=[
            jax.ShapeDtypeStruct((rows, width), jnp.bfloat16),
            jax.ShapeDtypeStruct((keys // 2, width), jnp.float32),
            jax.ShapeDtypeStruct((keys // 2, width), jnp.bfloat16),
            jax.ShapeDtypeStruct((keys // 2, width), jnp.float32),
            jax.ShapeDtypeStruct((keys // 2, width), jnp.bfloat16),
        ],
        scratch_shapes=[
            pltpu.VMEM((blocks, keys, block_rows), jnp.float32),
            pltpu.VMEM((2 * HD, keys), jnp.bfloat16),
            pltpu.VMEM((keys, 2 * HD), jnp.float32),
            pltpu.VMEM((keys, 2 * HD), jnp.float32),
        ],
        cost_estimate=pl.CostEstimate(
            flops=40 * rows * keys * width, transcendentals=12 * rows * keys, bytes_accessed=1 << 24
        ),
        name="attend_backward",
    )(query_rows, key_rows, value_rows, grad_rows, totals, query_docs[None], key_docs[:, None])


def body(
    hidden_in,
    doc_starts,
    query_weight,
    query_bias,
    key_weight,
    value_weight,
    value_bias,
    out_weight,
    out_bias,
    first_gain,
    first_shift,
    up_weight,
    up_bias,
    down_weight,
    down_bias,
    second_gain,
    second_shift,
    grad_out,
    *,
    count,
):
    low_type = jnp.bfloat16
    wide_type = jnp.float32
    place = lax.axis_index("seq")
    core = place % 2
    across = place // 2
    shard_index = lax.axis_index("shard")
    sequences, part_len, model_width = hidden_in.shape
    full_len = 4 * part_len

    mine = lax.dynamic_index_in_dim(hidden_in, across, 0, False)
    yours = lax.dynamic_index_in_dim(hidden_in, 1 - across, 0, False)
    came_low = flip_x(yours.astype(low_type))
    rows_low = jnp.concatenate([mine.astype(low_type), came_low], 0)
    all_low = jnp.concatenate([rows_low, flip_core(rows_low)], 0)
    rest = flip_x((yours - yours.astype(low_type).astype(wide_type)).astype(low_type))
    token_rows = jnp.concatenate(
        [mine, came_low.astype(wide_type) + rest.astype(wide_type)], 0
    )

    shards = jnp.concatenate([query_weight, key_weight, value_weight], 1).astype(low_type)
    joined = gather_weight(shards, count, core, across, False)
    vectors = (
        query_bias, value_bias, out_bias, first_gain, first_shift,
        down_bias, second_gain, second_shift,
    )
    packed = jnp.stack([item.astype(low_type) for item in vectors])
    packed = jnp.concatenate([packed, up_bias.astype(low_type).reshape(4, -1)], 0)
    packed = gather_shard(packed, count)
    vector_rows = [
        packed[:, i].reshape(-1).astype(wide_type) for i in range(len(vectors))
    ]
    (
        query_offset, value_offset, out_offset, first_scale, first_offset,
        down_offset, second_scale, second_offset,
    ) = vector_rows
    up_offset = packed[:, len(vectors):].reshape(-1).astype(wide_type)
    out_matrix = gather_weight(out_weight.astype(low_type), count, core, across, False)
    up_matrix = gather_weight(up_weight.astype(low_type), count, core, across, True)
    down_matrix = gather_weight(down_weight.astype(low_type), count, core, across, False)

    grad_mine = lax.dynamic_index_in_dim(grad_out, across, 0, False)
    grad_yours = lax.dynamic_index_in_dim(grad_out, 1 - across, 0, False)
    incoming = jnp.concatenate([grad_mine, flip_x(grad_yours)], 0)

    query_matrix = joined[:, :model_width]
    key_matrix = joined[:, model_width : 2 * model_width]
    value_matrix = joined[:, 2 * model_width :]
    query_rows = (product(rows_low, query_matrix) + query_offset).astype(low_type)
    key_rows = product(all_low, key_matrix).astype(low_type)
    value_rows = (product(all_low, value_matrix) + value_offset).astype(low_type)

    starts = lax.dynamic_index_in_dim(doc_starts, across, 0, True)
    doc_ids = document_ids(starts, full_len)[0]

    def docs_at(which_core):
        first = lax.dynamic_slice_in_dim(
            doc_ids, (2 * across + which_core) * part_len, part_len
        )
        second = lax.dynamic_slice_in_dim(
            doc_ids, (2 * (1 - across) + which_core) * part_len, part_len
        )
        return jnp.concatenate([first, second])

    query_docs = docs_at(core)
    key_docs = jnp.concatenate([query_docs, docs_at(1 - core)])
    context_rows, totals = attend_forward(
        query_rows, key_rows, value_rows, query_docs, key_docs
    )
    attended = product(context_rows, out_matrix) + out_offset
    normed, unit_one, inv_one = norm_forward(token_rows + attended, first_scale, first_offset)
    normed_low = normed.astype(low_type)
    up_values = product(normed_low, up_matrix) + up_offset
    activated = gelu_value(up_values).astype(low_type)
    down_values = product(activated, down_matrix) + down_offset
    result_rows, unit_two, inv_two = norm_forward(
        normed + down_values, second_scale, second_offset
    )

    def give_back(rows):
        own, other = rows[:part_len], flip_x(rows[part_len:])
        return place_pair(own[None], other[None], across == 1, 0)

    hidden_out = give_back(result_rows)

    grad_sum, grad_second_gain, grad_second_shift = norm_backward(
        incoming, unit_two, inv_two, second_scale
    )
    grad_down = grad_sum.astype(low_type)
    grad_down_bias = column_sum(grad_down)

    def start(name, grad, x_first):
        live[name] = start_grad(grad, count)
        plans[name] = stage_names(count, x_first)

    def post(name):
        parts[name] = send_stage(live[name], plans[name].pop(0), count, core, across)

    def take(*names):
        for name in names:
            live[name] = add_low(*parts.pop(name))

    live, plans, parts = {}, {}, {}
    start("down", weight_grad(activated, grad_down), True)
    post("down")
    grad_up = (product_back(grad_down, down_matrix) * gelu_slope(up_values)).astype(low_type)
    grad_up, parts["down"] = tie(grad_up, parts["down"])
    take("down")
    post("down")
    start("up", weight_grad(normed_low, grad_up), False)
    post("up")
    grad_up_bias = column_sum(grad_up)
    grad_normed = grad_sum + product_back(grad_up, up_matrix)
    grad_mixed, grad_first_gain, grad_first_shift = norm_backward(
        grad_normed, unit_one, inv_one, first_scale
    )
    grad_attended = grad_mixed.astype(low_type)
    grad_attended, parts["up"] = tie(grad_attended, parts["up"])
    take("up")
    post("up")
    start("out", weight_grad(context_rows, grad_attended), True)
    post("out")
    grad_out_bias = column_sum(grad_attended)
    grad_context = product_back(grad_attended, out_matrix).astype(low_type)
    pairs = model_width // (2 * HD)
    first_pairs = pairs // 2
    grad_context, parts["out"] = tie(grad_context, parts["out"])
    take("out")
    post("out")
    grads_one = attend_backward(
        query_rows, key_rows, value_rows, grad_context, totals, query_docs, key_docs,
        0, first_pairs,
    )
    grads_one, parts, grad_context = tie(grads_one, parts, grad_context)
    take("down", "up", "out")
    early = reduce_vector(
        jnp.concatenate(
            [
                grad_second_gain, grad_second_shift, grad_down_bias, grad_first_gain,
                grad_first_shift, grad_out_bias, grad_up_bias,
            ]
        ).reshape(-1, model_width),
        count,
    )
    post("down")
    post("up")
    post("out")
    grads_two = attend_backward(
        query_rows, key_rows, value_rows, grad_context, totals, query_docs, key_docs,
        first_pairs, pairs - first_pairs,
    )
    grads_two, parts, early = tie(grads_two, parts, early)
    take("down", "up", "out")
    grad_queries = jnp.concatenate([grads_one[0], grads_two[0]], 1)
    own_key, other_key, own_value, other_value = [
        jnp.concatenate([grads_one[i], grads_two[i]], 1) for i in range(1, 5)
    ]
    came = flip_core(jnp.concatenate([other_key, other_value], 0))
    split = other_key.shape[0]
    grad_keys = (own_key + came[:split].astype(wide_type)).astype(low_type)
    grad_values = (own_value + came[split:].astype(wide_type)).astype(low_type)
    start(
        "late",
        weight_grad(rows_low, jnp.concatenate([grad_queries, grad_keys, grad_values], 1)),
        True,
    )
    post("late")
    post("down")
    post("up")
    post("out")
    grad_rows = (
        grad_mixed
        + product_back(grad_queries, query_matrix)
        + product_back(grad_keys, key_matrix)
        + product_back(grad_values, value_matrix)
    )
    grad_rows, parts = tie(grad_rows, parts)
    grad_in = give_back(grad_rows)
    take("late", "down", "up", "out")
    post("late")
    late = reduce_vector(
        jnp.stack([column_sum(grad_queries), column_sum(grad_values)]), count
    )
    for name in ("down", "up", "out", "late"):
        while plans[name]:
            if name in parts:
                take(name)
            post(name)
        if name in parts:
            take(name)
    owned_down, owned_up, owned_out = spread_owned(
        [live["down"], live["up"], live["out"]], core, across
    )
    (owned_late,) = spread_owned([live["late"]], core, across)
    owned_query = owned_late[:, :model_width]
    owned_key = owned_late[:, model_width : 2 * model_width]
    owned_value = owned_late[:, 2 * model_width :]

    def owned_part(vector):
        size = vector.shape[0] // count
        return lax.dynamic_slice_in_dim(vector, shard_index * size, size)

    return (
        hidden_out,
        grad_in,
        owned_query,
        owned_part(late[0]),
        owned_key,
        owned_value,
        owned_part(late[1]),
        owned_out,
        owned_part(early[5]),
        owned_part(early[3]),
        owned_part(early[4]),
        owned_up,
        owned_part(early[6:].reshape(-1)),
        owned_down,
        owned_part(early[2]),
        owned_part(early[0]),
        owned_part(early[1]),
    )


def solution(mesh):
    placed = (
        P("shard", "seq", None),
        P("shard", None),
        P("shard", None),
        P("shard"),
        P("shard", None),
        P("shard", None),
        P("shard"),
        P("shard", None),
        P("shard"),
        P("shard"),
        P("shard"),
        P("shard", None),
        P("shard"),
        P("shard", None),
        P("shard"),
        P("shard"),
        P("shard"),
        P("shard", "seq", None),
    )
    return jax.shard_map(
        functools.partial(body, count=mesh.shape["shard"]),
        mesh=mesh,
        in_specs=placed,
        out_specs=(
            P("shard", "seq", None),
            P("shard", "seq", None),
            P("shard", None),
            P("shard"),
            P("shard", None),
            P("shard", None),
            P("shard"),
            P("shard", None),
            P("shard"),
            P("shard"),
            P("shard"),
            P("shard", None),
            P("shard"),
            P("shard", None),
            P("shard"),
            P("shard"),
            P("shard"),
        ),
        check_vma=False,
    )
```
